32 devices in a mesh: px: 8 (over z, y), py: 4 (over x, core).
Axes of the slice: x: 2, y: 2, z: 4, core: 2. Of those that a mesh axis runs over, the one named last changes fastest.
Arguments:
- flow_field: bfloat16 [64, 128, 128, 128], P(None, 'px', 'py'), may hold values from -6 to 6
- cotangent: bfloat16 [64, 128, 128, 128], P(None, 'px', 'py'), may hold values from -6 to 6
- tucker_core: float32 [16, 16, 8, 8, 8], replicated, may hold values from -6 to 6
- in_factor: float32 [64, 16], replicated, may hold values from -0.75 to 0.75
- out_factor: float32 [64, 16], replicated, may hold values from -1.5 to 1.5
- first_factor: float32 [32, 8], replicated, may hold values from -2 to 2
- second_factor: float32 [32, 8], replicated, may hold values from -2 to 2
- third_factor: float32 [32, 8], replicated, may hold values from -2 to 2
Outputs:
- output_field: bfloat16 [64, 128, 128, 128], P(None, 'px', 'py')
- core_grad: float32 [16, 16, 8, 8, 8], replicated
- in_grad: float32 [64, 16], replicated
- out_grad: float32 [64, 16], replicated
- first_grad: float32 [32, 8], replicated
- second_grad: float32 [32, 8], replicated
- third_grad: float32 [32, 8], replicated
The draws below stay inside these ranges and needn't reach their ends.
All inputs are finite; a program needn't handle non-finite values.
Results may differ from the reference program's by a relative error of at most 0.001.
Values sent between devices are 32-bit elements; how exact they have to be, the bound alone decides.
A program may use at most 192 MiB of HBM per device.

```python
import jax
import jax.numpy as jnp
from jax import lax

C = 64
NX = 128
NY = 128
NZ = 128
M1 = 32
M2 = 32
M3 = 32
RI = 16
RO = 16
R1 = 8
R2 = 8
R3 = 8


def block_scale(rng, extent, cuts, low, high):
    def one(position, shards_of):
        heights = jax.random.uniform(jax.random.fold_in(jax.random.fold_in(rng, 6), position), (shards_of,), jnp.float32, low / len(cuts), high / len(cuts))
        return jnp.repeat(jnp.exp(heights), extent[position] // shards_of).reshape((-1,) + (1,) * (len(extent) - position - 1))

    level = one(*cuts[0])
    for cut in cuts[1:]:
        level = level * one(*cut)
    return level


def centred(rng, shape, width, bound, pieces=(), kind=jnp.bfloat16):
    result = jax.random.normal(rng, shape, jnp.float32) * width
    if len(pieces) > 0:
        result = block_scale(rng, shape, pieces, -0.22, 0.18) * result
    return jnp.clip(result, min=-bound, max=bound).astype(kind)


def setup_inputs(seed: int = 0) -> dict:
    key_list = jax.random.split(jax.random.key(seed), 9)
    flow_field = centred(key_list[0], (C, NX, NY, NZ), 1.0, 6.0, ((1, 8), (2, 4)))
    cotangent = centred(key_list[1], (C, NX, NY, NZ), 1.0, 6.0, ((1, 8), (2, 4)))
    tucker_core = centred(key_list[2], (RI, RO, R1, R2, R3), (0.3 * ((NX * NY * NZ) // (2 * M1 * M2 * M3)) ** 0.5), 6.0, (), jnp.float32)
    in_factor = centred(key_list[3], (C, RI), C ** -0.5, 0.75, (), jnp.float32)
    out_factor = centred(key_list[4], (C, RO), RO ** -0.5, 1.5, (), jnp.float32)
    first_factor = centred(key_list[5], (M1, R1), R1 ** -0.5, 2.0, (), jnp.float32)
    second_factor = centred(key_list[6], (M2, R2), R2 ** -0.5, 2.0, (), jnp.float32)
    third_factor = centred(key_list[7], (M3, R3), R3 ** -0.5, 2.0, (), jnp.float32)
    return dict(flow_field=flow_field, cotangent=cotangent, tucker_core=tucker_core, in_factor=in_factor, out_factor=out_factor, first_factor=first_factor, second_factor=second_factor, third_factor=third_factor)


HIGHEST = lax.Precision.HIGHEST

def kept_index(count, length):
    half_count = count // 2
    return jnp.concatenate([jnp.arange(half_count), jnp.arange(length - half_count, length)]).astype(jnp.int32)

def spectrum(plane):
    whole = jnp.fft.rfftn(plane, axes=(0, 1, 2))
    rows_kept = kept_index(M1, NX)
    cols_kept = kept_index(M2, NY)
    trimmed = whole[rows_kept][:, cols_kept][:, :, :M3]
    return jnp.stack([jnp.real(trimmed), jnp.imag(trimmed)])

def to_grid(modes):
    values = modes[0] + 1j * modes[1]
    whole = jnp.zeros((NX, NY, NZ // 2 + 1), values.dtype)
    rows_kept = kept_index(M1, NX)
    cols_kept = kept_index(M2, NY)
    depth_kept = jnp.arange(M3).astype(jnp.int32)
    whole = whole.at[rows_kept[:, None, None], cols_kept[None, :, None], depth_kept[None, None, :]].set(values)
    return jnp.fft.irfftn(whole, s=(NX, NY, NZ), axes=(0, 1, 2))

def mixing(tucker_core, in_factor, out_factor, first_factor, second_factor, third_factor, spectra):
    partial_core = jnp.einsum('abrst,mt->abrsm', tucker_core, third_factor, precision=HIGHEST)
    partial_core = jnp.einsum('abrsm,ks->abrkm', partial_core, second_factor, precision=HIGHEST)
    kernel = jnp.einsum('abrkm,jr->abjkm', partial_core, first_factor, precision=HIGHEST)
    lifted = jnp.einsum('ia,ipjkm->apjkm', in_factor, spectra, precision=HIGHEST)
    mixed = jnp.einsum('abjkm,apjkm->bpjkm', kernel, lifted, precision=HIGHEST)
    return jnp.einsum('ob,bpjkm->opjkm', out_factor, mixed, precision=HIGHEST)

def reference(flow_field, cotangent, tucker_core, in_factor, out_factor, first_factor, second_factor, third_factor):
    spectra = lax.map(lambda plane: spectrum(plane.astype(jnp.float32)), flow_field)
    weights = jnp.where(jnp.arange(M3) == 0, 1.0, 2.0).astype(jnp.float32)
    inverse_count = 1.0 / (NX * NY * NZ)
    back = lax.map(lambda plane: spectrum(plane.astype(jnp.float32)), cotangent) * (weights * inverse_count)

    def forward(core_arg, in_arg, out_arg, first_arg, second_arg, third_arg):
        return mixing(core_arg, in_arg, out_arg, first_arg, second_arg, third_arg, spectra)
    joined, pullback = jax.vjp(forward, tucker_core, in_factor, out_factor, first_factor, second_factor, third_factor)
    grads = pullback(back)
    output_field = lax.map(lambda modes: to_grid(modes).astype(jnp.bfloat16), joined)
    return (output_field, grads[0], grads[1], grads[2], grads[3], grads[4], grads[5])
```

```python
import functools
import math

import jax
import jax.numpy as jnp
import numpy as np
from jax import lax
from jax.experimental import pallas as pl
from jax.experimental.pallas import tpu as pltpu
from jax.sharding import PartitionSpec as P

NX = 128
NY = 128
NZ = 128
M1 = 32
M2 = 32
M3 = 32


HIGHEST = lax.Precision.HIGHEST


def turn_table(count, length):
    position = jnp.arange(count)
    frequency = jnp.where(position < count // 2, position, position - count)
    cells_at = jnp.arange(length)
    phase = frequency[None, :] * cells_at[:, None] % length
    angle = 2.0 * math.pi / length * phase.astype(jnp.float32)
    cosine = jnp.cos(angle)
    sine = jnp.sin(angle)
    upper = jnp.stack([cosine, -sine], axis=1)
    lower = jnp.stack([sine, cosine], axis=1)
    return jnp.stack([upper, lower])


def depth_table(length, count):
    cells_at = jnp.arange(length)
    frequency = jnp.arange(count)
    phase = cells_at[:, None] * frequency[None, :] % length
    angle = 2.0 * math.pi / length * phase.astype(jnp.float32)
    return jnp.concatenate([jnp.cos(angle), -jnp.sin(angle)], axis=1)


def to_modes(fields, depth_tables):
    across = turn_table(M2, NY)
    along = turn_table(M1, NX)
    spectra = []
    for member, z_table in zip(fields, depth_tables):
        channels, rows_here, cols_here, depth_len = member.shape
        flat = jnp.dot(member.reshape(-1, depth_len), z_table, precision=HIGHEST)
        spectra.append(flat.reshape(channels, rows_here, cols_here, 2, M3))
    members = lax.all_to_all(tuple(spectra), "py", split_axis=4, concat_axis=2, tiled=True)
    lines = tuple(
        (jnp.einsum("cxypm,pyqk->cxqkm", member, across, precision=HIGHEST) for member in members)
    )
    members = (
        lax.all_to_all(lines[0], "px", split_axis=3, concat_axis=1, tiled=True),
        lax.all_to_all(lines[1], "px", split_axis=3, concat_axis=1, tiled=True),
    )
    return tuple(
        (jnp.einsum("cxpkm,pxqj->cqjkm", member, along, precision=HIGHEST) for member in members)
    )


def to_space(modes, depth_weights):
    across = turn_table(M2, NY)
    along = turn_table(M1, NX)
    depth_base = depth_table(NZ, M3).T.reshape(2, M3, NZ)
    lines = tuple(
        (jnp.einsum("cqjkm,pxqj->cpxkm", member, along, precision=HIGHEST) for member in modes)
    )
    members = (
        lax.all_to_all(lines[0], "px", split_axis=2, concat_axis=3, tiled=True),
        lax.all_to_all(lines[1], "px", split_axis=2, concat_axis=3, tiled=True),
    )
    columns = tuple(
        (jnp.einsum("cqxkm,pyqk->cpxym", member, across, precision=HIGHEST) for member in members)
    )
    members = (
        lax.all_to_all(columns[0], "py", split_axis=3, concat_axis=4, tiled=True),
        lax.all_to_all(columns[1], "py", split_axis=3, concat_axis=4, tiled=True),
    )
    return tuple(
        (
            jnp.einsum(
                "cpxyk,pkn->cxyn", member, depth_base * weight_row[None, :, None], precision=HIGHEST
            )
            for member, weight_row in zip(members, depth_weights)
        )
    )


def shards(
    flow_field,
    cotangent,
    tucker_core,
    in_factor,
    out_factor,
    first_factor,
    second_factor,
    third_factor,
):
    inverse_count = 1.0 / (NX * NY * NZ)
    weights = jnp.where(jnp.arange(M3) == 0, 1.0, 2.0).astype(jnp.float32)
    unit_weights = jnp.ones((M3,), jnp.float32)
    base_table = depth_table(NZ, M3)
    weighted_table = base_table * jnp.concatenate([weights, weights])[None, :]
    block_second = M2 // lax.axis_size("px")
    block_third = M3 // lax.axis_size("py")
    start_second = lax.axis_index("px") * block_second
    start_third = lax.axis_index("py") * block_third

    def build_kernel(core_arg, first_arg, second_arg, third_arg):
        second_rows = lax.dynamic_slice_in_dim(second_arg, start_second, block_second, 0)
        third_rows = lax.dynamic_slice_in_dim(third_arg, start_third, block_third, 0)
        partial_core = jnp.einsum("abrst,mt->abrsm", core_arg, third_rows, precision=HIGHEST)
        partial_core = jnp.einsum("abrsm,ks->abrkm", partial_core, second_rows, precision=HIGHEST)
        return jnp.einsum("abrkm,jr->abjkm", partial_core, first_arg, precision=HIGHEST)

    kernel, pullback = jax.vjp(build_kernel, tucker_core, first_factor, second_factor, third_factor)
    field_wide = flow_field.astype(jnp.float32)
    back_wide = cotangent.astype(jnp.float32)
    lifted_grid = jnp.einsum("cxyn,ca->axyn", field_wide, in_factor, precision=HIGHEST)
    back_grid = jnp.einsum("cxyn,cb->bxyn", back_wide, out_factor, precision=HIGHEST)
    lifted, back_mixed = to_modes((lifted_grid, back_grid), (base_table, weighted_table))
    back_mixed = back_mixed * inverse_count
    mixed = jnp.einsum("abjkm,apjkm->bpjkm", kernel, lifted, precision=HIGHEST)
    grad_kernel = jnp.einsum("bpjkm,apjkm->abjkm", back_mixed, lifted, precision=HIGHEST)
    back_lifted = jnp.einsum("abjkm,bpjkm->apjkm", kernel, back_mixed, precision=HIGHEST)
    mixed_grid, lifted_back = to_space((mixed, back_lifted), (weights, unit_weights))
    mixed_grid = mixed_grid * inverse_count
    output_field = jnp.einsum("ob,bxyn->oxyn", out_factor, mixed_grid, precision=HIGHEST).astype(
        jnp.bfloat16
    )
    grad_out = jnp.einsum("oxyn,bxyn->ob", back_wide, mixed_grid, precision=HIGHEST)
    grad_in = jnp.einsum("ixyn,axyn->ia", field_wide, lifted_back, precision=HIGHEST)
    grad_core, grad_first, grad_second, grad_third = pullback(grad_kernel)
    totals = lax.psum(
        (grad_core, grad_in, grad_out, grad_first, grad_second, grad_third), ("px", "py")
    )
    return (output_field, totals[0], totals[1], totals[2], totals[3], totals[4], totals[5])


BF16 = jnp.bfloat16
F32 = jnp.float32
NN = (((1,), (0,)), ((), ()))
NT = (((1,), (1,)), ((), ()))
TN = (((0,), (0,)), ((), ()))


def mul(a, b, dims=NN):
    return lax.dot_general(a, b, dims, preferred_element_type=F32)


def halves(x):
    high = x.astype(BF16)
    return high, (x - high.astype(F32)).astype(BF16)


def split(x):
    high = lax.reduce_precision(x, 8, 7)
    return high.astype(BF16), lax.reduce_precision(x - high, 8, 7).astype(BF16)


def mul3(a, b, dims=NN):
    (ah, al), (bh, bl) = a, b
    return mul(ah, bh, dims) + (mul(ah, bl, dims) + mul(al, bh, dims))


def np_halves(x):
    x = np.asarray(x, np.float32)
    high = x.astype(BF16)
    return jnp.asarray(high), jnp.asarray((x - high.astype(np.float32)).astype(BF16))


def np_turn(count, length):
    position = np.arange(count)
    frequency = np.where(position < count // 2, position, position - count)
    phase = frequency[None, :] * np.arange(length)[:, None] % length
    angle = 2.0 * np.pi / length * phase
    upper = np.stack([np.cos(angle), -np.sin(angle)], axis=1)
    lower = np.stack([np.sin(angle), np.cos(angle)], axis=1)
    return np.stack([upper, lower])


def np_depth(length, count, blocks):
    phase = np.arange(count)[:, None] * np.arange(length)[None, :] % length
    angle = 2.0 * np.pi / length * phase
    both = np.stack([np.cos(angle), -np.sin(angle)])
    both = both.reshape(2, blocks, count // blocks, length)
    return both.transpose(1, 0, 2, 3).reshape(2 * count, length)


def depth_modes(table, tile_ref, modes_ref, per):
    count = table.shape[0] // 2
    cells_here, length = tile_ref.shape[2], tile_ref.shape[3]

    def step(i, carry):
        two = tile_ref[pl.ds(2 * i, 2), 0].reshape(2 * cells_here, length)
        both = mul(table, two, NT)
        both = both[:count] + both[count:]
        for side in range(2):
            part = both[:, side * cells_here:(side + 1) * cells_here]
            row = pl.multiple_of((2 * i + side) * per, per)
            for g in range(count // per):
                modes_ref[g, pl.ds(row, per), :] = part[g * per:(g + 1) * per]
        return carry

    lax.fori_loop(0, tile_ref.shape[0] // 2, step, 0, unroll=8)


def lift_kernel(per, tile_ref, table_ref, wh_ref, wl_ref, out_ref, modes_ref):
    depth_modes(table_ref[...], tile_ref, modes_ref, per)
    weights = (wh_ref[...], wl_ref[...])
    blocks, parts = out_ref.shape[0], out_ref.shape[2]
    for b in range(blocks):
        for p in range(parts):
            out_ref[b, 0, p] = mul3(weights, halves(modes_ref[b * parts + p]))


def across_kernel(x_ref, th_ref, tl_ref, out_ref):
    blocks, parts = x_ref.shape[0], x_ref.shape[2]
    total = None
    for b in range(blocks):
        for p in range(parts):
            g = b * parts + p
            term = mul3((th_ref[g], tl_ref[g]), halves(x_ref[b, 0, p]), NT)
            total = term if total is None else total + term
    out_ref[...] = total.reshape(out_ref.shape)


def uncross_kernel(x_ref, th_ref, tl_ref, out_ref):
    rows = x_ref.shape[0] * x_ref.shape[2]
    lines = halves(x_ref[...].reshape(rows, x_ref.shape[3]).T)
    blocks, parts = out_ref.shape[0], out_ref.shape[2]
    for b in range(blocks):
        for p in range(parts):
            g = b * parts + p
            out_ref[b, 0, p] = mul3(lines, (th_ref[g], tl_ref[g]))


def mix_kernel(core_ref, fe_ref, se_ref, te_ref, lift_ref, back_ref,
               mixed_ref, backl_ref, gcore_ref, gf_ref, gs_ref, gt_ref,
               w_ref, k_ref, gk_ref, dw_ref):
    r1, modes = fe_ref.shape
    r2, r3 = se_ref.shape[0], te_ref.shape[0]
    ri, ro = lift_ref.shape[1], back_ref.shape[1]
    rest = r2 * r3
    pair = (se_ref[...][:, None, :] * te_ref[...][None, :, :]).reshape(rest, modes)
    for r in range(r1):
        w_ref[pl.ds(r * rest, rest), :] = pair * fe_ref[r:r + 1, :]
    weights = halves(w_ref[...])
    core = halves(core_ref[...])
    k_ref[...] = mul3(core, weights)
    for p in range(2):
        mixed = jnp.zeros((ro, modes), F32)
        for a in range(ri):
            block = k_ref[pl.ds(a * ro, ro), :]
            mixed = mixed + block * lift_ref[p, a:a + 1, :]
            backl_ref[p, a:a + 1, :] = jnp.sum(block * back_ref[p], axis=0, keepdims=True)
        mixed_ref[p] = mixed
    for a in range(ri):
        gk_ref[pl.ds(a * ro, ro), :] = (
            back_ref[0] * lift_ref[0, a:a + 1, :] + back_ref[1] * lift_ref[1, a:a + 1, :]
        )
    grad = halves(gk_ref[...])
    gcore_ref[...] = mul3(grad, weights, NT)
    dw_ref[...] = mul3(core, grad, TN)
    dpair = jnp.zeros((rest, modes), F32)
    for r in range(r1):
        dw = dw_ref[pl.ds(r * rest, rest), :]
        gf_ref[r:r + 1, :] = jnp.sum(dw * pair, axis=0, keepdims=True)
        dpair = dpair + dw * fe_ref[r:r + 1, :]
    dpair = dpair.reshape(r2, r3, modes)
    gs_ref[...] = jnp.sum(dpair * te_ref[...][None], axis=1)
    gt_ref[...] = jnp.sum(dpair * se_ref[...][:, None], axis=0)


def field_kernel(per, mixed_ref, table_ref, inv_h_ref, inv_l_ref, wh_ref, wl_ref, cot_ref,
                 out_ref, grad_ref, modes_ref):
    @pl.when(pl.program_id(0) == 0)
    def _():
        grad_ref[...] = jnp.zeros_like(grad_ref)

    depth_modes(table_ref[...], cot_ref, modes_ref, per)
    blocks, parts = mixed_ref.shape[0], mixed_ref.shape[2]
    weights = (wh_ref[...], wl_ref[...])
    total = None
    for b in range(blocks):
        for p in range(parts):
            g = b * parts + p
            spectrum = halves(mixed_ref[b, 0, p])
            term = mul3(halves(modes_ref[g]), spectrum, NT)
            total = term if total is None else total + term
    grad_ref[...] += total
    for b in range(blocks):
        for p in range(parts):
            modes_ref[b * parts + p] = mul3(weights, halves(mixed_ref[b, 0, p]))
    inverse = (inv_h_ref[...], inv_l_ref[...])
    groups = blocks * parts
    length = out_ref.shape[3]

    def step(i, carry):
        pieces = []
        for side in range(2):
            row = pl.multiple_of((2 * i + side) * per, per)
            for g in range(groups):
                pieces.append(modes_ref[g, pl.ds(row, per), :])
        lines = halves(jnp.concatenate(pieces, axis=0).T)
        both = mul3(lines, inverse)
        for side in range(2):
            out_ref[2 * i + side, 0] = both[:, side * length:(side + 1) * length].astype(BF16)
        return carry

    lax.fori_loop(0, out_ref.shape[0] // 2, step, 0, unroll=4)


def grad_kernel(per, back_ref, table_ref, tile_ref, grad_ref, modes_ref):
    @pl.when(pl.program_id(0) == 0)
    def _():
        grad_ref[...] = jnp.zeros_like(grad_ref)

    depth_modes(table_ref[...], tile_ref, modes_ref, per)
    blocks, parts = back_ref.shape[0], back_ref.shape[2]
    total = None
    for b in range(blocks):
        for p in range(parts):
            g = b * parts + p
            term = mul3(halves(modes_ref[g]), halves(back_ref[b, 0, p]), NT)
            total = term if total is None else total + term
    grad_ref[...] += total


def fast_shards(px, py, flow_field, cotangent, tucker_core, in_factor, out_factor,
                first_factor, second_factor, third_factor):
    channels, rows, cols, depth = flow_field.shape
    ri, ro, r1, r2, r3 = tucker_core.shape
    wide = 128 // cols
    tiles = rows // wide
    per = M3 // py
    keep = M2 // px
    lanes = wide * cols
    inverse_count = 1.0 / (NX * NY * NZ)

    base = np_depth(NZ, M3, py)
    weight = np.where(np.arange(M3) == 0, 1.0, 2.0).reshape(py, 1, per)
    weight = np.broadcast_to(weight, (py, 2, per)).reshape(-1, 1) * inverse_count
    table_f = jnp.concatenate(np_halves(base), axis=0)
    table_c = jnp.concatenate(np_halves(base * weight), axis=0)
    inv_h, inv_l = np_halves(np.kron(np.eye(2), base * weight))

    turn = np_turn(M2, NY).reshape(2, py, cols, 2, px, keep)
    across = np.einsum("psyoqk,xz->spqozkxy", turn, np.eye(wide))
    ah, al = np_halves(across.reshape(py * 2, px * 2 * wide * keep, lanes))
    turn = np_turn(M1, NX).reshape(2, px, tiles, wide, 2, M1)
    along = np.einsum("pstxoj,qk->oqjstpxk", turn, np.eye(keep))
    along = jnp.asarray(along.reshape(2 * keep * M1, px * tiles * 2 * wide * keep).astype(np.float32))

    eye = jnp.eye(per, dtype=F32)
    in_wide = split(jnp.einsum("ca,mn->amcn", in_factor, eye, precision=HIGHEST).reshape(ri * per, channels * per))
    out_back = split(jnp.einsum("cb,mn->bmcn", out_factor, eye, precision=HIGHEST).reshape(ro * per, channels * per))
    out_wide = split(jnp.einsum("cb,mn->cmbn", out_factor, eye, precision=HIGHEST).reshape(channels * per, ro * per))

    vmem = pl.BlockSpec(memory_space=pltpu.VMEM)
    field_spec = pl.BlockSpec((channels, 1, lanes, depth), lambda i: (0, i, 0, 0))
    mode_spec = pl.BlockSpec((py, 1, 2, ri * per, lanes), lambda i: (0, i, 0, 0, 0))
    line_spec = pl.BlockSpec((px, 1, 2 * wide * keep, ri * per), lambda i: (0, i, 0, 0))
    mode_shape = jax.ShapeDtypeStruct((py, tiles, 2, ri * per, lanes), F32)
    line_shape = jax.ShapeDtypeStruct((px, tiles, 2 * wide * keep, ri * per), F32)
    scratch = pltpu.VMEM((2 * py, channels * per, lanes), F32)
    params = pltpu.CompilerParams(vmem_limit_bytes=56 * 1024 * 1024)

    def cost(flops, moved):
        return pl.CostEstimate(flops=flops, bytes_accessed=moved, transcendentals=0)

    big = cost(4 * 10 ** 9, 20 * 10 ** 6)
    small = cost(10 ** 9, 8 * 10 ** 6)
    field = flow_field.reshape(channels, tiles, lanes, depth)
    cot = cotangent.reshape(channels, tiles, lanes, depth)

    def forward(tile, table, weights):
        return pl.pallas_call(
            functools.partial(lift_kernel, per), grid=(tiles,), out_shape=mode_shape,
            in_specs=[field_spec, vmem, vmem, vmem], out_specs=mode_spec,
            scratch_shapes=[scratch], compiler_params=params, cost_estimate=big,
        )(tile, table, *weights)

    def cross(modes):
        return pl.pallas_call(
            across_kernel, grid=(tiles,), out_shape=line_shape,
            in_specs=[mode_spec, vmem, vmem], out_specs=line_spec,
            compiler_params=params, cost_estimate=small,
        )(modes, ah, al)

    def uncross(lines):
        return pl.pallas_call(
            uncross_kernel, grid=(tiles,), out_shape=mode_shape,
            in_specs=[line_spec, vmem, vmem], out_specs=mode_spec,
            compiler_params=params, cost_estimate=small,
        )(lines, ah, al)

    def swap(x, name):
        flat = x.reshape(x.shape[0], -1, x.shape[-1])
        return lax.all_to_all(flat, name, split_axis=0, concat_axis=0, tiled=True).reshape(x.shape)

    modes = M1 * keep * per

    def spectra(x):
        lines = x.reshape(px * tiles * 2 * wide * keep, ri * per)
        s = jnp.dot(along, lines, precision=lax.Precision.HIGH)
        s = s.reshape(2, keep * M1, ri, per).transpose(0, 2, 1, 3)
        return s.reshape(2, ri, modes)

    def unspectra(s):
        s = s.reshape(2, ri, keep * M1, per).transpose(0, 2, 1, 3).reshape(2 * keep * M1, ri * per)
        lines = lax.dot_general(along, s, TN, precision=lax.Precision.HIGH)
        return lines.reshape(line_shape.shape)

    sent_f = swap(forward(field, table_f, in_wide), "py")
    sent_c = swap(forward(cot, table_c, out_back), "py")
    lifted = spectra(swap(cross(sent_f), "px"))
    back = spectra(swap(cross(sent_c), "px"))

    start_second = lax.axis_index("px") * keep
    start_third = lax.axis_index("py") * per
    second_rows = lax.dynamic_slice_in_dim(second_factor, start_second, keep, 0)
    third_rows = lax.dynamic_slice_in_dim(third_factor, start_third, per, 0)
    order = (keep, M1, per)
    fe = jnp.broadcast_to(first_factor.T[:, None, :, None], (r1,) + order).reshape(r1, modes)
    se = jnp.broadcast_to(second_rows.T[:, :, None, None], (r2,) + order).reshape(r2, modes)
    te = jnp.broadcast_to(third_rows.T[:, None, None, :], (r3,) + order).reshape(r3, modes)
    core = tucker_core.reshape(ri * ro, r1 * r2 * r3)
    ranks = r1 * r2 * r3
    shape = jax.ShapeDtypeStruct
    mixed, back_lifted, gcore, gf, gs, gt = pl.pallas_call(
        mix_kernel,
        out_shape=(
            shape((2, ro, modes), F32), shape((2, ri, modes), F32), shape((ri * ro, ranks), F32),
            shape((r1, modes), F32), shape((r2, modes), F32), shape((r3, modes), F32),
        ),
        in_specs=[vmem] * 6, out_specs=(vmem,) * 6,
        scratch_shapes=[
            pltpu.VMEM((ranks, modes), F32), pltpu.VMEM((ri * ro, modes), F32),
            pltpu.VMEM((ri * ro, modes), F32), pltpu.VMEM((ranks, modes), F32),
        ],
        compiler_params=params, cost_estimate=big,
    )(core, fe, se, te, lifted, back)
    grad_first = gf.reshape((r1,) + order).sum((1, 3)).T
    grad_second = gs.reshape((r2,) + order).sum((2, 3)).T
    grad_third = gt.reshape((r3,) + order).sum((1, 2)).T
    grad_second = lax.dynamic_update_slice_in_dim(jnp.zeros((M2, r2), F32), grad_second, start_second, 0)
    grad_third = lax.dynamic_update_slice_in_dim(jnp.zeros((M3, r3), F32), grad_third, start_third, 0)

    mixed = swap(uncross(swap(unspectra(mixed), "px")), "py")
    back_lifted = swap(uncross(swap(unspectra(back_lifted), "px")), "py")
    grad_shape = shape((channels * per, ro * per), F32)
    out, wide_out = pl.pallas_call(
        functools.partial(field_kernel, per), grid=(tiles,),
        out_shape=(shape(field.shape, BF16), grad_shape),
        in_specs=[mode_spec, vmem, vmem, vmem, vmem, vmem, field_spec],
        out_specs=(field_spec, vmem),
        scratch_shapes=[scratch], compiler_params=params, cost_estimate=big,
    )(mixed, table_c, inv_h, inv_l, *out_wide, cot)
    wide_in = pl.pallas_call(
        functools.partial(grad_kernel, per), grid=(tiles,), out_shape=grad_shape,
        in_specs=[mode_spec, vmem, field_spec], out_specs=vmem,
        scratch_shapes=[scratch], compiler_params=params, cost_estimate=big,
    )(back_lifted, table_f, field)

    def diagonal(g):
        g = g.reshape(channels, per, -1, per)
        return jnp.sum(g * eye[None, :, None, :], axis=(1, 3))

    totals = lax.psum(
        (gcore.reshape(tucker_core.shape), diagonal(wide_in), diagonal(wide_out),
         grad_first, grad_second, grad_third), ("px", "py")
    )
    return (out.reshape(flow_field.shape),) + tuple(totals)


def solution(mesh):
    px, py = mesh.shape["px"], mesh.shape["py"]
    cols, per = NY // py, M3 // py
    tidy = 128 % cols == 0 and per % 8 == 0 and (NX // px) % (128 // cols) == 0 and M2 % px == 0
    body = functools.partial(fast_shards, px, py) if tidy else shards
    return jax.shard_map(
        body,
        mesh=mesh,
        in_specs=(
            P(None, "px", "py", None),
            P(None, "px", "py", None),
            P(),
            P(),
            P(),
            P(),
            P(),
            P(),
        ),
        out_specs=(P(None, "px", "py", None), P(), P(), P(), P(), P(), P()),
        check_vma=False,
    )
```
